32 devices in a mesh: parts: 2 (over y), row: 4 (over z), col: 4 (over x, core), sub: 1.
Axes of the slice: x: 2, y: 2, z: 4, core: 2. Of those that a mesh axis runs over, the one named last changes fastest.
Arguments:
- activations: bfloat16 [1024, 2048], P(('parts', 'row'), ('col', 'sub')), parts along dimension 0, may hold values from -6 to 6
- expert_ids: int32 [1024, 8], P(('parts', 'row')), parts along dimension 0, may hold values from 0 to 15, all different within a row; in each aligned block of 32 rows (0 to 31, 32 to 63, ...) at most 32 rows name the same one
- gate_scores: float32 [1024, 8], P(('parts', 'row')), parts along dimension 0, may hold values from 0.05 to 0.5
- gate_proj: bfloat16 [16, 2048, 768], P(('row', 'col'), None, 'sub'), may hold values from -0.125 to 0.125
- up_proj: bfloat16 [16, 2048, 768], P(('row', 'col'), None, 'sub'), may hold values from -0.125 to 0.125
- down_proj: bfloat16 [16, 768, 2048], P(('row', 'col'), 'sub'), may hold values from -0.21875 to 0.21875
Outputs:
- moe_output: bfloat16 [1024, 2048], P(('parts', 'row'), ('col', 'sub')), parts along dimension 0
The draws below stay inside these ranges and needn't reach their ends.
There are 2 independent parts, one for each index of `parts`. The reference program is written for one: setup_inputs(seed, part) draws one part's arguments, and reference() takes and returns one part's arrays. A program takes and returns all parts, laid end to end along the dimension named above; an argument that names none is the same for every part. Nothing has to cross between parts.
Inputs may be any that keep to these rules, and one draw needn't show every extreme that they name: `expert_ids`: each row names 8 different experts. In each aligned block of 32 rows no expert is named by more than 32 rows, a bound that some block reaches.
All inputs are finite; a program needn't handle non-finite values.
Results may differ from the reference program's by a relative error of at most 0.0057.
Values may be sent and summed in bfloat16 or wider, within the bound.
No kernel may reach another device: no remote copies, remote signals or barrier semaphores. Data moves between devices by JAX's collectives and lax.ppermute only.
A program may use at most 64 MiB of HBM per device.

```python
import math
import jax
import jax.numpy as jnp
import numpy as np
from jax import lax

D = 2048
HID = 768
TOP = 8
E = 16
TOKENS = 512
BLOCK = 32
CAP = 32


def steps_of(own_key, extent, pieces, smallest, high):
    def one(position, shards_of):
        steps = jax.random.uniform(jax.random.fold_in(jax.random.fold_in(own_key, 6), position), (shards_of,), jnp.float32, smallest / len(pieces), high / len(pieces))
        return jnp.repeat(jnp.exp(steps), extent[position] // shards_of).reshape((-1,) + (1,) * (len(extent) - position - 1))

    gain = one(*pieces[0])
    for cut in pieces[1:]:
        gain = gain * one(*cut)
    return gain


def shared_out(stream_key, own, number, rows, number_of, top, reach, slope):
    ranking = jax.random.permutation(stream_key, number_of)
    heavy_load, usual = shares(number_of, rows * top, reach, slope, True), shares(number_of, rows * top, reach, slope, False)
    places = jnp.arange(number_of)

    def named(sizes, rotation):
        used = int((sizes > 0).sum())
        fixed = max(1, used // 4)
        passed = fixed + (places - fixed + rotation * (used - fixed)) % max(1, number_of - fixed)
        return jnp.zeros((number_of,), jnp.int32).at[ranking[jnp.where(places < fixed, places, passed)]].set(jnp.asarray(sizes, jnp.int32))

    sizes = jnp.where(number % 4 == 0, named(heavy_load, number // 4), named(usual, number - number // 4 - 1))
    mixed = jax.random.permutation(jax.random.fold_in(own, 3), number_of)
    giver, sink = mixed[0:number_of // 2 * 2:2], mixed[1:number_of // 2 * 2:2]
    slack = jnp.minimum(sizes[giver] - 1, reach - sizes[sink]) // 2
    slack = jnp.where((giver == ranking[0]) | (sink == ranking[0]) | (sizes[sink] == 0), 0, jnp.maximum(slack, 0))
    passed = jax.random.randint(jax.random.fold_in(own, 4), (number_of // 2,), 0, 1 << 20) % (slack + 1)
    sizes = sizes.at[giver].add(-passed).at[sink].add(passed)
    members = jnp.searchsorted(jnp.cumsum(sizes), jnp.arange(rows * top), side="right").astype(jnp.int32)
    grid = members.reshape(top, rows).T
    grid = grid[jax.random.permutation(jax.random.fold_in(own, 1), rows)]
    rotation = jax.random.randint(jax.random.fold_in(own, 2), (rows, 1), 0, top)
    return jnp.take_along_axis(grid, (jnp.arange(top)[None, :] + rotation) % top, axis=1)


def shares(amount, total, limit, lean, full):
    portions = [(1 << 20) // math.isqrt(grade ** lean) + 1 for grade in range(1, amount + 1)]
    largest = limit if full else min(limit, max(-(-total // amount), total * portions[0] // sum(portions)))
    least = 1 if total - largest >= amount - 1 else 0
    given, surplus = [largest] + [least] * (amount - 1), total - largest - least * (amount - 1)
    while surplus > 0:
        free = [i for i in range(1, amount) if given[i] < largest] or [i for i in range(1, amount) if given[i] < limit]
        mass, budget = sum([portions[i] for i in free]), surplus
        for i in free:
            more = min(limit - given[i], max(1, budget * portions[i] // mass), surplus)
            given[i] = given[i] + more
            surplus = surplus - more
    return np.array(given)


def normal_values(key, dims, deviation, limit, pieces=(), held_as=jnp.bfloat16):
    drawn = deviation * jax.random.normal(key, dims, jnp.float32)
    if pieces:
        drawn = drawn * steps_of(key, dims, pieces, -0.22, 0.18)
    return jnp.clip(drawn, -limit, limit).astype(held_as)


def setup_inputs(seed: int = 0, part: int = 0) -> dict:
    seeds = jax.random.split(jax.random.key(seed), 7)
    part_splits = jax.random.split(jax.random.fold_in(seeds[6], part), 7)
    activations = normal_values(part_splits[0], (TOKENS, D), 1.0, 6.0, ((0, 4), (1, 4)))
    expert_ids_keys = jax.random.split(jax.random.fold_in(part_splits[1], 1), TOKENS // BLOCK)
    expert_ids_turns = jax.random.permutation(jax.random.fold_in(part_splits[1], 3), TOKENS // BLOCK)
    expert_ids = jax.vmap(lambda own, number: shared_out(jax.random.fold_in(part_splits[1], 2), own, number, BLOCK, E, TOP, CAP, 2))(expert_ids_keys, expert_ids_turns).reshape((TOKENS, TOP))
    gate_scores = jnp.clip(jnp.exp(math.log(0.5) - 2.3025851 * jax.random.uniform(part_splits[2], (TOKENS, TOP), jnp.float32) ** steps_of(part_splits[2], (TOKENS, TOP), ((0, 4),), -0.2, 0.2)), 0.05, 0.5)
    gate_proj = normal_values(seeds[3], (E, D, HID), D ** -0.5, 0.125, ((0, 16),))
    up_proj = normal_values(seeds[4], (E, D, HID), D ** -0.5, 0.125, ((0, 16),))
    down_proj = normal_values(seeds[5], (E, HID, D), HID ** -0.5, 0.21875, ((0, 16),))
    return {"activations": activations, "expert_ids": expert_ids, "gate_scores": gate_scores, "gate_proj": gate_proj, "up_proj": up_proj, "down_proj": down_proj}


def reference(activations, expert_ids, gate_scores, gate_proj, up_proj, down_proj):
    blocks = TOKENS // BLOCK
    per_block = BLOCK * TOP
    grouped = expert_ids.reshape(blocks, per_block).astype(jnp.int32)
    numbers = jnp.arange(E, dtype=jnp.int32)
    onehot = (grouped[:, :, None] == numbers[None, None, :]).astype(jnp.int32)
    running = jnp.cumsum(onehot, axis=1).astype(jnp.int32) - 1
    slot_rank = jnp.sum(onehot * running, axis=2).astype(jnp.int32)
    block_ids = jnp.broadcast_to(jnp.arange(blocks, dtype=jnp.int32)[:, None], (blocks, per_block))
    assigned = jnp.arange(TOKENS * TOP, dtype=jnp.int32).reshape(blocks, per_block)
    slot_table = jnp.full((blocks, E, CAP), TOKENS * TOP, jnp.int32)
    slot_table = slot_table.at[block_ids, grouped, slot_rank].set(assigned)
    scores = jnp.concatenate([gate_scores.reshape(TOKENS * TOP), jnp.zeros((1,), jnp.float32)])
    padded = jnp.concatenate([activations, jnp.zeros((1, D), activations.dtype)], axis=0)

    def one_expert(summed, expert):
        slot_ids = lax.dynamic_index_in_dim(slot_table, expert, axis=1, keepdims=False).reshape(blocks * CAP)
        row_ids = (slot_ids // TOP).astype(jnp.int32)
        inputs = padded[row_ids]
        gate_val = jnp.dot(inputs, gate_proj[expert], preferred_element_type=jnp.float32)
        up_val = jnp.dot(inputs, up_proj[expert], preferred_element_type=jnp.float32)
        hidden = (jax.nn.silu(gate_val) * up_val).astype(jnp.bfloat16)
        rounded = jnp.dot(hidden, down_proj[expert], preferred_element_type=jnp.float32).astype(jnp.bfloat16)
        rounded = lax.optimization_barrier(rounded)
        result = rounded.astype(jnp.float32)
        summed = summed.at[row_ids].add(scores[slot_ids][:, None] * result)
        return summed, None

    summed, unused = lax.scan(one_expert, jnp.zeros((TOKENS + 1, D), jnp.float32), jnp.arange(E, dtype=jnp.int32))
    return summed[:TOKENS].astype(jnp.bfloat16)
```

```python
import functools
import math

import jax
import jax.numpy as jnp
from jax import lax
from jax.experimental import pallas as pl
from jax.experimental.pallas import tpu as pltpu
from jax.sharding import PartitionSpec as P

TOP = 8


def slot_places(chosen, experts, capacity):
    count = chosen.shape[0] * chosen.shape[1]
    flat_ids = chosen.reshape(count)
    onehot = (flat_ids[:, None] == jnp.arange(experts, dtype=jnp.int32)[None, :]).astype(jnp.int32)
    running = jnp.cumsum(onehot, axis=0) - 1
    ranking = jnp.sum(onehot * running, axis=1)
    return flat_ids * capacity + ranking


def fill_slots(row_block, places, experts, capacity, top_count):
    owners = jnp.full((experts * capacity,), row_block.shape[0], jnp.int32)
    owners = owners.at[places].set(jnp.arange(places.shape[0], dtype=jnp.int32) // top_count)
    padded = jnp.concatenate(
        [row_block, jnp.zeros((1, row_block.shape[1]), row_block.dtype)], axis=0
    )
    return padded[owners].reshape(experts, capacity, row_block.shape[1])


def run_expert(stacked, gate_proj, up_proj, down_proj):
    layout = stacked.shape
    inputs = stacked.reshape(-1, layout[-1])
    gate_val = jnp.dot(inputs, gate_proj[0], preferred_element_type=jnp.float32)
    up_val = jnp.dot(inputs, up_proj[0], preferred_element_type=jnp.float32)
    hidden = (jax.nn.silu(gate_val) * up_val).astype(jnp.bfloat16)
    partial_out = jnp.dot(hidden, down_proj[0], preferred_element_type=jnp.float32)
    return partial_out.reshape(layout)


def send_back(stacked, gate_proj, up_proj, down_proj):
    partial_out = run_expert(stacked, gate_proj, up_proj, down_proj)
    landed = lax.all_to_all(partial_out, ("row", "col"), split_axis=1, concat_axis=1, tiled=True)
    return lax.psum_scatter(landed, "sub", scatter_dimension=0, tiled=True).astype(jnp.bfloat16)


def routed(activations, expert_ids, gate_scores, gate_proj, up_proj, down_proj):
    col_count = lax.axis_size("col")
    sub_count = lax.axis_size("sub")
    experts = lax.axis_size("row") * col_count
    group_rows = expert_ids.shape[0]
    block_rows = group_rows // (col_count * sub_count)
    capacity = max(2, min(block_rows, 2 * block_rows * TOP // experts))
    quarter = sub_count * block_rows
    width = activations.shape[1] * col_count * sub_count
    whole = lax.all_gather(activations, ("col", "sub"), axis=1, tiled=True)
    col_start = lax.axis_index("col") * quarter
    sub_index = lax.axis_index("sub")
    my_rows = lax.dynamic_slice_in_dim(whole, col_start, quarter, 0)
    my_ids = lax.dynamic_slice_in_dim(expert_ids, col_start, quarter, 0)
    own_scores = lax.dynamic_slice_in_dim(
        gate_scores, col_start + sub_index * block_rows, block_rows, 0
    )
    places = []
    for member in range(sub_count):
        lower = member * block_rows
        places.append(slot_places(my_ids[lower : lower + block_rows], experts, capacity))
    own_places = lax.dynamic_index_in_dim(jnp.stack(places), sub_index, 0, keepdims=False)
    buffers = []
    for member in range(sub_count):
        lower = member * block_rows
        buffers.append(
            fill_slots(my_rows[lower : lower + block_rows], places[member], experts, capacity, TOP)
        )
    outgoing = jnp.stack(buffers)
    returned = send_back(
        lax.all_to_all(outgoing, ("row", "col"), split_axis=1, concat_axis=1, tiled=True),
        gate_proj,
        up_proj,
        down_proj,
    )
    picked = returned.reshape(-1, width)[own_places].reshape(block_rows, TOP, width)
    share = jnp.sum(own_scores[:, :, None] * picked.astype(jnp.float32), axis=1)
    return lax.all_to_all(
        share.astype(jnp.bfloat16), ("col", "sub"), split_axis=1, concat_axis=0, tiled=True
    )


def swap(value, axis, bit):
    count = lax.axis_size(axis)
    return lax.ppermute(value, axis, [(i, i ^ bit) for i in range(count)])


def expert_kernel(group, feats, place, *refs):
    blocks = len(group)
    tables, refs = refs[:blocks], refs[blocks:]
    xs, refs = refs[: blocks * feats], refs[blocks * feats :]
    gate, up, down, kept, sent, whole, hidden = refs
    col, expert = place[0], place[1].astype(jnp.float32)
    rows, depth = xs[0].shape
    units = gate.shape[1]
    tile = math.gcd(units, 256)
    for m in range(feats):
        start = pl.multiple_of((col ^ m) * depth, depth)
        for j in range(blocks):
            whole[j * rows : (j + 1) * rows, pl.ds(start, depth)] = xs[j * feats + m][...]
    for h in range(0, units, tile):
        g = jnp.dot(whole[...], gate[:, h : h + tile], preferred_element_type=jnp.float32)
        u = jnp.dot(whole[...], up[:, h : h + tile], preferred_element_type=jnp.float32)
        hidden[:, h : h + tile] = (g / (1.0 + jnp.exp(-g)) * u).astype(jnp.bfloat16)
    wide = []
    for j in range(blocks):
        ids, scores = tables[j][:TOP], tables[j][TOP:]
        weight = jnp.sum(jnp.where(ids == expert, scores, 0.0), axis=0, keepdims=True)
        wide.append(jnp.broadcast_to(weight, (128, rows)).T)
    wide = jnp.concatenate(wide, axis=0)
    wide = jnp.concatenate([wide] * (tile // 128), axis=1)
    for m in [*range(1, feats, 2), *range(0, feats, 2)]:
        target = sent if m & 1 else kept
        for n in range(0, depth, tile):
            start = pl.multiple_of((col ^ m) * depth + n, tile)
            y = jnp.dot(hidden[...], down[:, pl.ds(start, tile)], preferred_element_type=jnp.float32)
            place_in = m // 2 * depth + n
            target[:, place_in : place_in + tile] = (y * wide).astype(target.dtype)


def full_specs(count):
    return [pl.BlockSpec(memory_space=pltpu.VMEM)] * count


def run_expert_group(place, group, tables, xs, gate, up, down, feats):
    blocks = len(group)
    rows, depth = xs[0].shape
    units = gate.shape[1]
    out = (blocks * rows, feats // 2 * depth)
    return pl.pallas_call(
        functools.partial(expert_kernel, group, feats),
        out_shape=[jax.ShapeDtypeStruct(out, jnp.float32), jax.ShapeDtypeStruct(out, jnp.bfloat16)],
        in_specs=[pl.BlockSpec(memory_space=pltpu.SMEM)] + full_specs(blocks + 3 + len(xs)),
        out_specs=full_specs(2),
        scratch_shapes=[
            pltpu.VMEM((blocks * rows, feats * depth), jnp.bfloat16),
            pltpu.VMEM((blocks * rows, units), jnp.bfloat16),
        ],
        cost_estimate=pl.CostEstimate(
            flops=6 * blocks * rows * depth * feats * units, bytes_accessed=1 << 20, transcendentals=0
        ),
        compiler_params=pltpu.CompilerParams(vmem_limit_bytes=16 << 20),
        name="expert",
    )(place, *tables, *xs, gate, up, down)


def join_kernel(blocks, feats, kept, got, *outs):
    rows = outs[0].shape[0]
    depth = outs[0].shape[1]
    for j in range(blocks):
        for m in range(feats):
            at = (slice(j * rows, (j + 1) * rows), slice(m * depth, (m + 1) * depth))
            out = outs[j * feats + m]
            out[...] = (kept[at] + got[at].astype(jnp.float32)).astype(out.dtype)


def run_join(kept, got, blocks, feats):
    rows, depth = kept.shape[0] // blocks, kept.shape[1] // feats
    shapes = []
    for _ in range(blocks):
        for m in range(feats):
            shapes.append(jax.ShapeDtypeStruct((rows, depth), jnp.bfloat16 if m else jnp.float32))
    return pl.pallas_call(
        functools.partial(join_kernel, blocks, feats),
        out_shape=shapes,
        in_specs=full_specs(2),
        out_specs=full_specs(len(shapes)),
        cost_estimate=pl.CostEstimate(flops=kept.size, bytes_accessed=kept.size, transcendentals=0),
        compiler_params=pltpu.CompilerParams(vmem_limit_bytes=8 << 20),
        name="join",
    )(kept, got)


def sum_kernel(*refs):
    total = refs[0][...].astype(jnp.float32)
    for ref in refs[1:-1]:
        total += ref[...].astype(jnp.float32)
    refs[-1][...] = total.astype(refs[-1].dtype)


def run_sum(values, dtype):
    return pl.pallas_call(
        sum_kernel,
        out_shape=jax.ShapeDtypeStruct(values[0].shape, dtype),
        in_specs=full_specs(len(values)),
        out_specs=full_specs(1)[0],
        cost_estimate=pl.CostEstimate(
            flops=values[0].size * len(values), bytes_accessed=values[0].size, transcendentals=0
        ),
        compiler_params=pltpu.CompilerParams(vmem_limit_bytes=8 << 20),
        name="total",
    )(*values)


def dense(activations, expert_ids, gate_scores, gate_proj, up_proj, down_proj):
    row_count, col_count = lax.axis_size("row"), lax.axis_size("col")
    row, col = lax.axis_index("row"), lax.axis_index("col")
    place = jnp.stack([col, row * col_count + col]).astype(jnp.int32)
    packed = jnp.concatenate([expert_ids.astype(jnp.float32).T, gate_scores.T], axis=0)
    groups = [(0, 2), (1, 3)]
    far = col_count // 2
    order = [2, 1, 3]
    held = {(0, 0): activations}
    table = {0: packed}
    for j in order:
        held[j, 0] = swap(activations, "row", j)
    held[0, far] = swap(activations, "col", far)
    for j in order:
        table[j] = swap(packed, "row", j)
    results = []
    for group in groups:
        for j in group:
            if j:
                held[j, far] = swap(held[j, 0], "col", far)
        for m in (0, far):
            for j in group:
                held[j, m ^ 1] = swap(held[j, m], "col", 1)
    kept, sent, other = {}, {}, {}
    for group in groups:
        xs = [held[j, m] for j in group for m in range(col_count)]
        kept[group], sent[group] = run_expert_group(
            place, group, [table[j] for j in group], xs, gate_proj[0], up_proj[0], down_proj[0], col_count
        )
    total = {}
    for group in groups:
        got = swap(sent[group], "col", 1)
        joined = run_join(kept[group], got, len(group), 2)
        for i, j in enumerate(group):
            total[j] = (joined[2 * i], swap(joined[2 * i + 1], "col", far))
    for j in order:
        total[j] = (swap(run_sum(total[j], jnp.bfloat16), "row", j),)
    return run_sum([*total[0], *total[1], *total[2], *total[3]], jnp.bfloat16)


def per_device(activations, expert_ids, gate_scores, gate_proj, up_proj, down_proj):
    row_count, col_count, sub_count = lax.axis_size("row"), lax.axis_size("col"), lax.axis_size("sub")
    block_rows = expert_ids.shape[0] // (col_count * sub_count)
    every_row = block_rows * row_count * col_count <= 2 * block_rows * TOP * 1
    whole = sub_count == 1 and col_count > 1
    squares = row_count & (row_count - 1) == 0 and col_count & (col_count - 1) == 0
    chosen = dense if every_row and whole and squares else routed
    return chosen(activations, expert_ids, gate_scores, gate_proj, up_proj, down_proj)


def solution(mesh):
    placed = (
        P(("parts", "row"), ("col", "sub")),
        P(("parts", "row"), None),
        P(("parts", "row"), None),
        P(("row", "col"), None, "sub"),
        P(("row", "col"), None, "sub"),
        P(("row", "col"), "sub", None),
    )
    return jax.shard_map(
        per_device,
        mesh=mesh,
        in_specs=placed,
        out_specs=P(("parts", "row"), ("col", "sub")),
        check_vma=False,
    )
```
